32 devices in a mesh: fsdp: 8 (over z, x), tp: 4 (over y, core).
Axes of the slice: x: 2, y: 2, z: 4, core: 2. Of those that a mesh axis runs over, the one named last changes fastest.
Arguments:
- x_saved: bfloat16 [2048, 5120], P('fsdp'), may hold values from -6 to 6
- grad_out: bfloat16 [2048, 5120], P('fsdp', 'tp'), may hold values from -0.125 to 0.125
- projection: bfloat16 [5120, 256], replicated, may hold values from -0.375 to 0.375
- master_weight: float32 [5120, 5120], P('fsdp', 'tp'), may hold values from -0.078125 to 0.078125
- momentum: float32 [5120, 5120], P('fsdp', 'tp'), may hold values from -6 to 6
- x_next: bfloat16 [2048, 5120], P('fsdp'), may hold values from -6 to 6
Outputs:
- new_master: float32 [5120, 5120], P('fsdp', 'tp')
- new_momentum: float32 [5120, 5120], P('fsdp', 'tp')
- next_out: bfloat16 [2048, 5120], P('fsdp', 'tp')
The draws below stay inside these ranges and needn't reach their ends.
All inputs are finite; a program needn't handle non-finite values.
Results may differ from the reference program's by a relative error of at most 0.0062.
Values may be sent and summed in bfloat16 or wider, within the bound.
No kernel may reach another device: no remote copies, remote signals or barrier semaphores. Data moves between devices by JAX's collectives and lax.ppermute only.
A program may use at most 64 MiB of HBM per device.

```python
import jax
import jax.numpy as jnp

D = 5120
R = 256
TOKENS = 2048


def block_levels(key, shape, cuts, least, top_value):
    loudness = 1.0
    for dim, parts in cuts:
        steps = jax.random.uniform(jax.random.fold_in(jax.random.fold_in(key, 6), dim), (parts,), jnp.float32, least / len(cuts), top_value / len(cuts))
        loudness = loudness * jnp.repeat(jnp.exp(steps), shape[dim] // parts).reshape((-1,) + (1,) * (len(shape) - 1 - dim))
    return loudness


def gaussian(rng, extent, width, limit, split=(), kind=jnp.bfloat16):
    entries = jax.random.normal(rng, extent, jnp.float32) * width
    if len(split) > 0:
        entries = block_levels(rng, extent, split, -0.22, 0.18) * entries
    return jnp.clip(entries, min=-limit, max=limit).astype(kind)


def setup_inputs(seed: int = 0) -> dict:
    key_of = jax.random.split(jax.random.key(seed), 7)
    return {
        "x_saved": gaussian(key_of[0], (TOKENS, D), 1.0, 6.0, ((0, 8),)),
        "grad_out": gaussian(key_of[1], (TOKENS, D), TOKENS ** -0.5, 0.125, ((0, 8), (1, 4))),
        "projection": gaussian(key_of[2], (D, R), R ** -0.5, 0.375),
        "master_weight": gaussian(key_of[3], (D, D), D ** -0.5, 0.078125, ((0, 8), (1, 4)), jnp.float32),
        "momentum": gaussian(key_of[4], (D, D), 1.0, 6.0, ((0, 8), (1, 4)), jnp.float32),
        "x_next": gaussian(key_of[5], (TOKENS, D), 1.0, 6.0, ((0, 8),)),
    }


def reference(x_saved, grad_out, projection, master_weight, momentum, x_next):
    projected = jnp.dot(x_saved, projection, preferred_element_type=jnp.float32).astype(jnp.bfloat16)
    sketch = jnp.dot(grad_out.T, projected, preferred_element_type=jnp.float32)
    sketch_b = sketch.astype(jnp.bfloat16)
    decompressed = jnp.dot(projection, sketch_b.T, preferred_element_type=jnp.float32)
    new_momentum = 0.9 * momentum + decompressed
    new_master = master_weight - 0.01 * new_momentum
    base_b = (master_weight - 0.009 * momentum).astype(jnp.bfloat16)
    next_proj = jnp.dot(x_next, projection, preferred_element_type=jnp.float32).astype(jnp.bfloat16)
    full_part = jnp.dot(x_next, base_b, preferred_element_type=jnp.float32)
    low_part = jnp.dot(next_proj, sketch_b.T, preferred_element_type=jnp.float32)
    next_out = (full_part - 0.01 * low_part).astype(jnp.bfloat16)
    return new_master, new_momentum, next_out
```

```python
import jax
import jax.numpy as jnp
from jax import lax
from jax.sharding import PartitionSpec as P


F32 = jnp.float32
BF16 = jnp.bfloat16
LANES = 128
LINE_LIMIT = 8


def dot(a, b):
    return jnp.dot(a, b, preferred_element_type=F32)


def dot_t(a, b):
    return lax.dot_general(a, b, (((1,), (1,)), ((), ())), preferred_element_type=F32)


def partial_sketch_of(x_saved, grad_out, projection):
    projected = dot(x_saved, projection).astype(BF16)
    return lax.dot_general(grad_out, projected, (((0,), (0,)), ((), ())), preferred_element_type=F32)


def gathered(x_saved, grad_out, projection, master_weight, momentum, x_next):
    base_b = (master_weight - 0.009 * momentum).astype(BF16)
    full_part = dot(x_next, lax.all_gather(base_b, "fsdp", axis=0, tiled=True))
    partial_sketch = partial_sketch_of(x_saved, grad_out, projection)
    sketch_b = lax.psum(partial_sketch, "fsdp").astype(BF16)
    rows = master_weight.shape[0]
    proj_rows = lax.dynamic_slice_in_dim(projection, lax.axis_index("fsdp") * rows, rows, 0)
    new_momentum = 0.9 * momentum + dot_t(proj_rows, sketch_b)
    new_master = master_weight - 0.01 * new_momentum
    next_proj = dot(x_next, projection).astype(BF16)
    next_out = (full_part - 0.01 * dot_t(next_proj, sketch_b)).astype(BF16)
    return new_master, new_momentum, next_out


def split_columns(cols, parts):
    units = cols // LANES
    if cols % LANES or units < parts:
        return [(0, cols)]
    edges = [LANES * (units * j // parts) for j in range(parts + 1)]
    return [(a, b - a) for a, b in zip(edges, edges[1:])]


def make_line(depth, tp, parts):
    pair = 2
    fsdp = depth * pair
    half = depth // 2
    bits = tp.bit_length() - 1

    def send(a, moves):
        return lax.ppermute(a, "fsdp", [(i * pair + x, j * pair + x) for i, j in moves for x in range(pair)])

    def swap(a):
        return lax.ppermute(a, "fsdp", [(i, i ^ 1) for i in range(fsdp)])

    def ordered(first, mine, other):
        a = jnp.concatenate([mine, other], 0)
        b = jnp.concatenate([other, mine], 0)
        return jnp.where(first, a, b)

    def line(x_saved, grad_out, projection, master_weight, momentum, x_next):
        me = lax.axis_index("fsdp")
        z, x = me // pair, me % pair
        t = lax.axis_index("tp")
        rows, cols = master_weight.shape
        tokens = x_next.shape[0]
        share = tokens // tp
        slot = sum(((t >> b) & 1) << (bits - 1 - b) for b in range(bits)) if bits else 0

        def columns(row0, count, block):
            mine = lax.dynamic_slice(x_next, (row0, (block * pair + x) * rows), (count, rows))
            other = lax.dynamic_slice(x_next, (row0, (block * pair + 1 - x) * rows), (count, rows))
            return jnp.concatenate([mine, other], 1)

        pieces = {}
        for s in range(depth - 1, 0, -1):
            piece = columns(slot * share, share, (z + s) % depth)
            pieces[s] = send(piece, [(i, (i + s) % depth) for i in range(depth)])

        base_b = (master_weight - 0.009 * momentum).astype(BF16)
        spans = split_columns(cols, parts)
        others = [swap(lax.slice_in_dim(base_b, c, c + w, axis=1)) for c, w in spans]

        partial_sketch = partial_sketch_of(x_saved, grad_out, projection)
        hrows = cols // pair
        kept = lax.dynamic_slice_in_dim(partial_sketch, x * hrows, hrows, 0)
        given = lax.dynamic_slice_in_dim(partial_sketch, (1 - x) * hrows, hrows, 0)
        acc = kept + swap(given.astype(BF16)).astype(F32)

        blocks = {}
        for s in pieces:
            cur = pieces[s]
            for b in range(bits - 1, -1, -1):
                got = lax.ppermute(cur, "tp", [(i, i ^ (1 << b)) for i in range(tp)])
                cur = ordered(((t >> b) & 1) == 0, cur, got)
            blocks[s] = cur
        blocks[0] = columns(0, tokens, z)

        for k in range(1, half):
            acc = acc + send(acc.astype(BF16), [(k - 1, k), (depth - k, depth - k - 1)]).astype(F32)
        mine = acc.astype(BF16)
        total = (mine.astype(F32) + send(mine, [(half - 1, half), (half, half - 1)]).astype(F32)).astype(BF16)
        for k in range(half - 1, 0, -1):
            got = send(total, [(k, k - 1), (depth - k - 1, depth - k)])
            total = jnp.where((z == k - 1) | (z == depth - k), got, total)
        sketch_b = ordered(x == 0, total, swap(total))

        next_proj = dot(x_next, projection).astype(BF16)
        outs = []
        for (c, w), other in zip(spans, others):
            weight = jnp.concatenate([lax.slice_in_dim(base_b, c, c + w, axis=1), other], 0)
            part = {s: dot(blocks[s], weight) for s in blocks}
            down = up = None
            for k in range(1, depth):
                a, b = part[depth - k], part[k]
                if down is not None:
                    a, b = a + down.astype(F32), b + up.astype(F32)
                down = send(a.astype(BF16), [(i, i - 1) for i in range(depth - k, depth)])
                up = send(b.astype(BF16), [(i, i + 1) for i in range(k)])
            low = dot_t(next_proj, lax.slice_in_dim(sketch_b, c, c + w, axis=0))
            outs.append((part[0] + down.astype(F32) + up.astype(F32) - 0.01 * low).astype(BF16))

        proj_rows = lax.dynamic_slice_in_dim(projection, me * rows, rows, 0)
        new_momentum = 0.9 * momentum + dot_t(proj_rows, sketch_b)
        new_master = master_weight - 0.01 * new_momentum
        return new_master, new_momentum, jnp.concatenate(outs, 1)

    return line


def solution(mesh):
    fsdp, tp = mesh.shape["fsdp"], mesh.shape["tp"]
    depth = fsdp // 2
    line_fits = fsdp % 4 == 0 and depth <= LINE_LIMIT and tp & (tp - 1) == 0
    body = make_line(depth, tp, 5) if line_fits else gathered
    placed = (
        P("fsdp", None),
        P("fsdp", "tp"),
        P(),
        P("fsdp", "tp"),
        P("fsdp", "tp"),
        P("fsdp", None),
    )
    return jax.shard_map(
        body,
        mesh=mesh,
        in_specs=placed,
        out_specs=(P("fsdp", "tp"), P("fsdp", "tp"), P("fsdp", "tp")),
        check_vma=False,
    )
```

```python
import jax
import jax.numpy as jnp
from jax import lax
from jax.sharding import PartitionSpec as P


F32 = jnp.float32
BF16 = jnp.bfloat16
LANES = 128


def dot(a, b):
    return jnp.dot(a, b, preferred_element_type=F32)


def dot_t(a, b):
    return lax.dot_general(a, b, (((1,), (1,)), ((), ())), preferred_element_type=F32)


def partial_sketch_of(x_saved, grad_out, projection):
    projected = dot(x_saved, projection).astype(BF16)
    return lax.dot_general(grad_out, projected, (((0,), (0,)), ((), ())), preferred_element_type=F32)


def gathered(x_saved, grad_out, projection, master_weight, momentum, x_next):
    base_b = (master_weight - 0.009 * momentum).astype(BF16)
    full_part = dot(x_next, lax.all_gather(base_b, "fsdp", axis=0, tiled=True))
    partial_sketch = partial_sketch_of(x_saved, grad_out, projection)
    sketch_b = lax.psum(partial_sketch, "fsdp").astype(BF16)
    rows = master_weight.shape[0]
    proj_rows = lax.dynamic_slice_in_dim(projection, lax.axis_index("fsdp") * rows, rows, 0)
    new_momentum = 0.9 * momentum + dot_t(proj_rows, sketch_b)
    new_master = master_weight - 0.01 * new_momentum
    next_proj = dot(x_next, projection).astype(BF16)
    next_out = (full_part - 0.01 * dot_t(next_proj, sketch_b)).astype(BF16)
    return new_master, new_momentum, next_out


def split_columns(cols, weights):
    units = cols // LANES
    total = sum(weights)
    if cols % LANES or units < total:
        return [(0, cols)]
    edges, seen = [0], 0
    for w in weights:
        seen += w
        edges.append(LANES * (units * seen // total))
    return [(a, b - a) for a, b in zip(edges, edges[1:])]


DEPTH = 4
PAIR = 2
CHUNKS = (1, 2, 2)


def make_line(tp):
    bits = tp.bit_length() - 1

    def send(a, moves, name):
        with jax.named_scope(name):
            return lax.ppermute(a, "fsdp", [(i * PAIR + x, j * PAIR + x) for i, j in moves for x in range(PAIR)])

    def swap(a, name):
        with jax.named_scope(name):
            return lax.ppermute(a, "fsdp", [(i, i ^ 1) for i in range(DEPTH * PAIR)])

    def swap_tp(a, b, name):
        with jax.named_scope(name):
            return lax.ppermute(a, "tp", [(i, i ^ (1 << b)) for i in range(tp)])

    def ordered(first, mine, other, axis):
        a = jnp.concatenate([mine, other], axis)
        b = jnp.concatenate([other, mine], axis)
        return jnp.where(first, a, b)

    def line(x_saved, grad_out, projection, master_weight, momentum, x_next):
        me = lax.axis_index("fsdp")
        z, x = me // PAIR, me % PAIR
        t = lax.axis_index("tp")
        rows, cols = master_weight.shape
        tokens = x_next.shape[0]
        share = tokens // tp
        slot = sum(((t >> b) & 1) << (bits - 1 - b) for b in range(bits)) if bits else 0

        def columns(row0, count, block):
            mine = lax.dynamic_slice(x_next, (row0, (block * PAIR + x) * rows), (count, rows))
            other = lax.dynamic_slice(x_next, (row0, (block * PAIR + 1 - x) * rows), (count, rows))
            return jnp.concatenate([mine, other], 1)

        spans = split_columns(cols, CHUNKS)
        bases = [
            (master_weight[:, c : c + w] - 0.009 * momentum[:, c : c + w]).astype(BF16) for c, w in spans
        ]
        others = [swap(b, f"w{j}") for j, b in enumerate(bases)]

        pieces = {}
        for s in (3, 1, 2):
            piece = columns(slot * share, share, (z + s) % DEPTH)
            pieces[s] = send(piece, [(i, (i + s) % DEPTH) for i in range(DEPTH)], f"xz{s}")
        blocks = {0: columns(0, tokens, z)}
        for group in ((3, 1), (2,)):
            cur = jnp.stack([pieces[s] for s in group])
            for b in range(bits - 1, -1, -1):
                got = swap_tp(cur, b, f"xt{b}_{group[0]}")
                cur = ordered(((t >> b) & 1) == 0, cur, got, 1)
            for n, s in enumerate(group):
                blocks[s] = cur[n]

        partial_sketch = partial_sketch_of(x_saved, grad_out, projection)
        hrows = cols // PAIR
        kept = lax.dynamic_slice_in_dim(partial_sketch, x * hrows, hrows, 0)
        given = lax.dynamic_slice_in_dim(partial_sketch, (1 - x) * hrows, hrows, 0)
        acc = kept + swap(given.astype(BF16), "sx").astype(F32)
        acc = acc + send(acc.astype(BF16), [(0, 1), (3, 2)], "s1").astype(F32)
        mine = acc.astype(BF16)
        total = (mine.astype(F32) + send(mine, [(1, 2), (2, 1)], "s2").astype(F32)).astype(BF16)
        got = send(total, [(1, 0), (2, 3)], "s3")
        total = jnp.where((z == 0) | (z == 3), got, total)
        sketch_b = ordered(x == 0, total, swap(total, "sg"), 0)

        next_proj = dot(x_next, projection).astype(BF16)
        down = [(1, 0), (2, 1), (3, 2)]
        up = [(0, 1), (1, 2), (2, 3)]
        outs = []
        for j, (c, w) in enumerate(spans):
            weight = jnp.concatenate([bases[j], others[j]], 0)
            part = {s: dot(blocks[s], weight) for s in blocks}
            far = send(jnp.where(z >= 2, part[3], part[1]).astype(BF16), [(3, 2), (0, 1)], f"a{j}")
            near_d = send(part[1].astype(BF16), down, f"d{j}")
            near_u = send(part[3].astype(BF16), up, f"u{j}")
            two = send((part[2] + far.astype(F32)).astype(BF16), [(i, (i + 2) % DEPTH) for i in range(DEPTH)], f"b{j}")
            low = dot_t(next_proj, lax.slice_in_dim(sketch_b, c, c + w, axis=0))
            full = part[0] + near_d.astype(F32) + near_u.astype(F32) + two.astype(F32)
            outs.append((full - 0.01 * low).astype(BF16))

        proj_rows = lax.dynamic_slice_in_dim(projection, me * rows, rows, 0)
        new_momentum = 0.9 * momentum + dot_t(proj_rows, sketch_b)
        new_master = master_weight - 0.01 * new_momentum
        return new_master, new_momentum, jnp.concatenate(outs, 1)

    return line


def solution(mesh):
    fsdp, tp = mesh.shape["fsdp"], mesh.shape["tp"]
    body = make_line(tp) if fsdp == DEPTH * PAIR and tp & (tp - 1) == 0 else gathered
    placed = (
        P("fsdp", None),
        P("fsdp", "tp"),
        P(),
        P("fsdp", "tp"),
        P("fsdp", "tp"),
        P("fsdp", None),
    )
    return jax.shard_map(
        body,
        mesh=mesh,
        in_specs=placed,
        out_specs=(P("fsdp", "tp"), P("fsdp", "tp"), P("fsdp", "tp")),
        check_vma=False,
    )
```

```python
import jax
import jax.numpy as jnp
from jax import lax
from jax.sharding import PartitionSpec as P


F32 = jnp.float32
BF16 = jnp.bfloat16
LANES = 128


def dot(a, b):
    return jnp.dot(a, b, preferred_element_type=F32)


def dot_t(a, b):
    return lax.dot_general(a, b, (((1,), (1,)), ((), ())), preferred_element_type=F32)


def partial_sketch_of(x_saved, grad_out, projection):
    projected = dot(x_saved, projection).astype(BF16)
    return lax.dot_general(grad_out, projected, (((0,), (0,)), ((), ())), preferred_element_type=F32)


def gathered(x_saved, grad_out, projection, master_weight, momentum, x_next):
    base_b = (master_weight - 0.009 * momentum).astype(BF16)
    full_part = dot(x_next, lax.all_gather(base_b, "fsdp", axis=0, tiled=True))
    partial_sketch = partial_sketch_of(x_saved, grad_out, projection)
    sketch_b = lax.psum(partial_sketch, "fsdp").astype(BF16)
    rows = master_weight.shape[0]
    proj_rows = lax.dynamic_slice_in_dim(projection, lax.axis_index("fsdp") * rows, rows, 0)
    new_momentum = 0.9 * momentum + dot_t(proj_rows, sketch_b)
    new_master = master_weight - 0.01 * new_momentum
    next_proj = dot(x_next, projection).astype(BF16)
    next_out = (full_part - 0.01 * dot_t(next_proj, sketch_b)).astype(BF16)
    return new_master, new_momentum, next_out


def split_columns(cols, weights):
    units = cols // LANES
    total = sum(weights)
    if cols % LANES or units < total:
        return [(0, cols)]
    edges, seen = [0], 0
    for w in weights:
        seen += w
        edges.append(LANES * (units * seen // total))
    return [(a, b - a) for a, b in zip(edges, edges[1:])]


DEPTH = 4
PAIR = 2
CHUNKS = (2, 2, 1)


def make_line(tp):
    bits = tp.bit_length() - 1

    def swap(a, step, name):
        with jax.named_scope(name):
            return lax.ppermute(a, "fsdp", [(i, i ^ step) for i in range(DEPTH * PAIR)])

    def swap_tp(a, step, name):
        with jax.named_scope(name):
            return lax.ppermute(a, "tp", [(i, i ^ step) for i in range(tp)])

    def line(x_saved, grad_out, projection, master_weight, momentum, x_next):
        me = lax.axis_index("fsdp")
        z, x = me // PAIR, me % PAIR
        t = lax.axis_index("tp")
        rows, cols = master_weight.shape
        tokens = x_next.shape[0]
        share = tokens // tp

        def columns(row0, count, block):
            mine = lax.dynamic_slice(x_next, (row0, (block * PAIR + x) * rows), (count, rows))
            other = lax.dynamic_slice(x_next, (row0, (block * PAIR + 1 - x) * rows), (count, rows))
            return jnp.concatenate([mine, other], 1)

        def true_rows(a):
            parts = []
            for q in range(tp):
                off = t ^ q
                at = sum(((off >> b) & 1) << (bits - 1 - b) for b in range(bits)) if bits else 0
                parts.append(lax.dynamic_slice_in_dim(a, at * share, share, 0))
            return jnp.concatenate(parts, 0)

        spans = split_columns(cols, CHUNKS)
        bases = [
            (master_weight[:, c : c + w] - 0.009 * momentum[:, c : c + w]).astype(BF16) for c, w in spans
        ]
        others = [swap(b, 1, f"w{j}") for j, b in enumerate(bases)]

        pieces = {r: swap(columns(t * share, share, z ^ r), r * PAIR, f"xz{r}") for r in (3, 1, 2)}
        blocks = {0: columns(0, tokens, z)}
        for group in ((3, 1), (2,)):
            cur = jnp.stack([pieces[r] for r in group])
            for b in range(bits - 1, -1, -1):
                cur = jnp.concatenate([cur, swap_tp(cur, 1 << b, f"xt{b}_{group[0]}")], 1)
            for n, r in enumerate(group):
                blocks[r] = cur[n]

        partial_sketch = partial_sketch_of(x_saved, grad_out, projection)
        hrows = cols // PAIR
        kept = lax.dynamic_slice_in_dim(partial_sketch, x * hrows, hrows, 0)
        given = lax.dynamic_slice_in_dim(partial_sketch, (1 - x) * hrows, hrows, 0)
        acc = kept + swap(given.astype(BF16), 1, "sx").astype(F32)
        for r in (1, 2):
            mine = acc.astype(BF16)
            acc = mine.astype(F32) + swap(mine, r * PAIR, f"sz{r}").astype(F32)
        total = acc.astype(BF16)
        got = swap(total, 1, "sg")
        sketch_b = jnp.where(x == 0, jnp.concatenate([total, got]), jnp.concatenate([got, total]))

        next_proj = dot(x_next, projection).astype(BF16)
        outs = []
        for j, (c, w) in enumerate(spans):
            weight = lax.optimization_barrier(jnp.concatenate([bases[j], others[j]], 0))
            near = jnp.stack([dot(blocks[r], weight).astype(BF16) for r in (1, 3)])
            near = swap(near, PAIR, f"a{j}")
            two = swap((dot(blocks[2], weight) + near[1].astype(F32)).astype(BF16), 2 * PAIR, f"b{j}")
            full = dot(blocks[0], weight) + true_rows(near[0].astype(F32) + two.astype(F32))
            low = dot_t(next_proj, lax.slice_in_dim(sketch_b, c, c + w, axis=0))
            outs.append((full - 0.01 * low).astype(BF16))

        proj_rows = lax.dynamic_slice_in_dim(projection, me * rows, rows, 0)
        new_momentum = 0.9 * momentum + dot_t(proj_rows, sketch_b)
        new_master = master_weight - 0.01 * new_momentum
        return new_master, new_momentum, jnp.concatenate(outs, 1)

    return line


def solution(mesh):
    fsdp, tp = mesh.shape["fsdp"], mesh.shape["tp"]
    body = make_line(tp) if fsdp == DEPTH * PAIR and tp & (tp - 1) == 0 else gathered
    placed = (
        P("fsdp", None),
        P("fsdp", "tp"),
        P(),
        P("fsdp", "tp"),
        P("fsdp", "tp"),
        P("fsdp", None),
    )
    return jax.shard_map(
        body,
        mesh=mesh,
        in_specs=placed,
        out_specs=(P("fsdp", "tp"), P("fsdp", "tp"), P("fsdp", "tp")),
        check_vma=False,
    )
```
